32 devices in a mesh: gx: 2 (over x), gy: 4 (over y, core), gz: 4 (over z).
Axes of the slice: x: 2, y: 2, z: 4, core: 2. Of those that a mesh axis runs over, the one named last changes fastest.
Arguments:
- velocity: float32 [3, 32, 64, 512], P(None, 'gx', 'gy', 'gz'), may hold values from -6 to 6
- gradients: bfloat16 [2, 3, 32, 64, 512], P(None, None, 'gx', 'gy', 'gz'), may hold values from -6 to 6
- shift_x: int32 [2, 4, 8, 4], P(None, 'gx', 'gy', 'gz'), may hold values from -6 to 6
- shift_y: int32 [2, 4, 8, 4], P(None, 'gx', 'gy', 'gz'), may hold values from -6 to 6
- shift_z: int32 [2, 4, 8, 4], P(None, 'gx', 'gy', 'gz'), may hold values from -14 to 14
- fractions: int32 [2, 3, 4, 8, 4], P(None, None, 'gx', 'gy', 'gz'), may hold values from 0 to 7
Outputs:
- hess_vec: float32 [3, 32, 64, 512], P(None, 'gx', 'gy', 'gz')
The draws below stay inside these ranges and needn't reach their ends.
All inputs are finite; a program needn't handle non-finite values.
Results may differ from the reference program's by a relative error of at most 0.0003.
Values sent between devices are 32-bit elements; how exact they have to be, the bound alone decides.
A program may use at most 64 MiB of HBM per device.

```python
import jax
import jax.numpy as jnp
from jax import lax

BX = 8
BY = 8
BZ = 128
RX = 6
RY = 6
RZ = 14
STEPS = 2
NX = 32
NY = 64
NZ = 512
NBX = 4
NBY = 8
NBZ = 4


def set_ends(array, rng, smallest, largest):
    place = [jax.random.randint(jax.random.fold_in(rng, axis), (), 0, length) for axis, length in enumerate(array.shape)]
    main_axis = array.shape.index(max(array.shape))
    neighbour = place[:main_axis] + [(place[main_axis] + 1) % array.shape[main_axis]] + place[main_axis + 1:]
    return array.at[tuple(place)].set(smallest).at[tuple(neighbour)].set(largest)


def level_of(rng, dims, pieces, least, high):
    loudness = 1.0
    for axis_at, blocks in pieces:
        heights = jax.random.uniform(jax.random.fold_in(jax.random.fold_in(rng, 6), axis_at), (blocks,), jnp.float32, least / len(pieces), high / len(pieces))
        loudness = loudness * jnp.repeat(jnp.exp(heights), dims[axis_at] // blocks).reshape((-1,) + (1,) * (len(dims) - 1 - axis_at))
    return loudness


def gaussian(own_key, shape, spread, bound, cuts=(), kind=jnp.bfloat16):
    array = jax.random.normal(own_key, shape, jnp.float32) * spread
    if len(cuts) > 0:
        array = level_of(own_key, shape, cuts, -0.22, 0.18) * array
    return jnp.clip(array, min=-bound, max=bound).astype(kind)


def setup_inputs(seed: int = 0) -> dict:
    seeds = jax.random.split(jax.random.key(seed), 7)
    velocity = gaussian(seeds[0], (3, NX, NY, NZ), 1.0, 6.0, ((1, 2), (2, 4), (3, 4)), jnp.float32)
    gradients = gaussian(seeds[1], (STEPS, 3, NX, NY, NZ), 1.0, 6.0, ((2, 2), (3, 4), (4, 4)))
    shift_x = set_ends(jax.random.randint(seeds[2], (STEPS, NBX, NBY, NBZ), 0 - RX, RX + 1), jax.random.fold_in(seeds[2], 1), 0 - RX, RX).astype(jnp.int32)
    shift_y = set_ends(jax.random.randint(seeds[3], (STEPS, NBX, NBY, NBZ), 0 - RY, RY + 1), jax.random.fold_in(seeds[3], 1), 0 - RY, RY).astype(jnp.int32)
    shift_z = set_ends(jax.random.randint(seeds[4], (STEPS, NBX, NBY, NBZ), 0 - RZ, RZ + 1), jax.random.fold_in(seeds[4], 1), 0 - RZ, RZ).astype(jnp.int32)
    fractions = set_ends(jax.random.randint(seeds[5], (STEPS, 3, NBX, NBY, NBZ), 0, 8), jax.random.fold_in(seeds[5], 1), 0, 7).astype(jnp.int32)
    return {"velocity": velocity, "gradients": gradients, "shift_x": shift_x, "shift_y": shift_y, "shift_z": shift_z, "fractions": fractions}


STEP_SIZE = 0.5
REG_WEIGHT = 0.1
LAPLACE_TAPS = (-205.0 / 72.0, 8.0 / 5.0, -1.0 / 5.0, 8.0 / 315.0, -1.0 / 560.0)


def cubic_weights(fractions):
    fraction = fractions.astype(jnp.float32) / 8.0
    squared = fraction * fraction
    cubed = squared * fraction
    taps = jnp.stack([0.5 * (2.0 * squared - cubed - fraction), 0.5 * (3.0 * cubed - 5.0 * squared + 2.0), 0.5 * (4.0 * squared - 3.0 * cubed + fraction), 0.5 * (cubed - squared)], axis=-1)
    return taps.reshape(3, -1, 4)


def block_starts(shift_x, shift_y, shift_z):
    count_x, count_y, count_z = shift_x.shape
    base_x = jnp.arange(count_x, dtype=jnp.int32)[:, None, None] * BX
    base_y = jnp.arange(count_y, dtype=jnp.int32)[None, :, None] * BY
    base_z = jnp.arange(count_z, dtype=jnp.int32)[None, None, :] * BZ
    start_x = (base_x + shift_x + (RX + 1)).astype(jnp.int32).reshape(-1)
    start_y = (base_y + shift_y + (RY + 1)).astype(jnp.int32).reshape(-1)
    start_z = (base_z + shift_z + (RZ + 1)).astype(jnp.int32).reshape(-1)
    return start_x, start_y, start_z


def apply_cubic(window, weight_x, weight_y, weight_z):
    span_z = window.shape[2] - 3
    along_z = sum(weight_z[a] * window[:, :, a:a + span_z] for a in range(4))
    span_y = window.shape[1] - 3
    along_y = sum(weight_y[a] * along_z[:, a:a + span_y, :] for a in range(4))
    span_x = window.shape[0] - 3
    return sum(weight_x[a] * along_y[a:a + span_x] for a in range(4))


def transpose_cubic(values, weight_x, weight_y, weight_z):
    along_x = sum(weight_x[a] * jnp.pad(values, ((a, 3 - a), (0, 0), (0, 0))) for a in range(4))
    along_y = sum(weight_y[a] * jnp.pad(along_x, ((0, 0), (a, 3 - a), (0, 0))) for a in range(4))
    return sum(weight_z[a] * jnp.pad(along_y, ((0, 0), (0, 0), (a, 3 - a))) for a in range(4))


def to_blocks(field):
    tile_x, tile_y, tile_z = field.shape
    split = field.reshape(tile_x // BX, BX, tile_y // BY, BY, tile_z // BZ, BZ)
    return split.transpose(0, 2, 4, 1, 3, 5).reshape(-1, BX, BY, BZ)


def from_blocks(blocks, tile_x, tile_y, tile_z):
    split = blocks.reshape(tile_x // BX, tile_y // BY, tile_z // BZ, BX, BY, BZ)
    return split.transpose(0, 3, 1, 4, 2, 5).reshape(tile_x, tile_y, tile_z)


def spread_blocks(field, start_x, start_y, start_z, weights):
    values = to_blocks(field)
    accumulated = jnp.zeros((field.shape[0] + 2 * (RX + 2), field.shape[1] + 2 * (RY + 2), field.shape[2] + 2 * (RZ + 2)), jnp.float32)

    def add_block(b, accumulated):
        window = transpose_cubic(values[b], weights[0, b], weights[1, b], weights[2, b])
        corner = (start_x[b], start_y[b], start_z[b])
        current = lax.dynamic_slice(accumulated, corner, window.shape)
        return lax.dynamic_update_slice(accumulated, current + window, corner)

    return lax.fori_loop(0, values.shape[0], add_block, accumulated)


def neg_laplacian(padded):
    tile_x = padded.shape[1] - 8
    tile_y = padded.shape[2] - 8
    tile_z = padded.shape[3] - 8

    def shifted(off_x, off_y, off_z):
        return padded[:, 4 + off_x:4 + off_x + tile_x, 4 + off_y:4 + off_y + tile_y, 4 + off_z:4 + off_z + tile_z]

    result = (3.0 * LAPLACE_TAPS[0]) * shifted(0, 0, 0)
    for k in range(1, 5):
        result = result + LAPLACE_TAPS[k] * (shifted(k, 0, 0) + shifted(-k, 0, 0) + shifted(0, k, 0) + shifted(0, -k, 0) + shifted(0, 0, k) + shifted(0, 0, -k))
    return -result


def advect(field, shift_x, shift_y, shift_z, fractions):
    padded = jnp.pad(field, ((RX + 2, RX + 2), (RY + 2, RY + 2), (RZ + 2, RZ + 2)))
    start_x, start_y, start_z = block_starts(shift_x, shift_y, shift_z)
    weights = cubic_weights(fractions)

    def one_block(block_items):
        corner_x, corner_y, corner_z, weight_x, weight_y, weight_z = block_items
        window = lax.dynamic_slice(padded, (corner_x, corner_y, corner_z), (BX + 3, BY + 3, BZ + 3))
        return apply_cubic(window, weight_x, weight_y, weight_z)

    blocks = lax.map(one_block, (start_x, start_y, start_z, weights[0], weights[1], weights[2]))
    return from_blocks(blocks, field.shape[0], field.shape[1], field.shape[2])


def advect_transposed(field, shift_x, shift_y, shift_z, fractions):
    start_x, start_y, start_z = block_starts(shift_x, shift_y, shift_z)
    weights = cubic_weights(fractions)
    accumulated = spread_blocks(field, start_x, start_y, start_z, weights)
    return accumulated[RX + 2:RX + 2 + field.shape[0], RY + 2:RY + 2 + field.shape[1], RZ + 2:RZ + 2 + field.shape[2]]


def reference(velocity, gradients, shift_x, shift_y, shift_z, fractions):
    state = jnp.zeros(velocity.shape[1:], jnp.float32)
    for k in range(STEPS):
        source = state + STEP_SIZE * jnp.sum(gradients[k].astype(jnp.float32) * velocity, axis=0)
        state = advect(source, shift_x[k], shift_y[k], shift_z[k], fractions[k])
    adjoint = state
    gauss_term = jnp.zeros_like(velocity)
    for k in reversed(range(STEPS)):
        adjoint = advect_transposed(adjoint, shift_x[k], shift_y[k], shift_z[k], fractions[k])
        gauss_term = gauss_term + STEP_SIZE * gradients[k].astype(jnp.float32) * adjoint[None]
    faces = jnp.pad(velocity, ((0, 0), (4, 4), (4, 4), (4, 4)))
    regular = REG_WEIGHT * neg_laplacian(faces)
    return regular + gauss_term
```

```python
import functools

import jax
import jax.numpy as jnp
from jax import lax
from jax.experimental import pallas as pl
from jax.experimental.pallas import tpu as pltpu
from jax.sharding import PartitionSpec as P

BX = 8
BY = 8
BZ = 128
RX = 6
RY = 6
RZ = 14
STEPS = 2

STEP_SIZE = 0.5
REG_WEIGHT = 0.1
LAPLACE_TAPS = (-205.0 / 72.0, 8.0 / 5.0, -1.0 / 5.0, 8.0 / 315.0, -1.0 / 560.0)

HX = RX + 2
HY = RY + 2
HZ = RZ + 2
LANES = 128
WIDE = 2 * HZ
PK = LANES // WIDE
XG = HX // PK
LH = 4
VPK = LANES // (2 * LH)
WX = BX + 2 * HX
WY = BY + 2 * HY
MESH = pl.DeviceIdType.MESH


def kernel(shape, vel, grad, shx, shy, shz, frac, out,
           E0, E1, U, T, YP, XP, ACC0, ACC1, BU, ST, ADJ,
           S, RZD, RZU, YRD, YRU, XPD, XPU, XMD, XMU, ZS, ZRD, ZRU,
           VE, YSU, YSD, YVD, YVU, SV, VRD, VRU, send, recv):
    TX, TY, TZ = vel.shape[1:]
    NBX, NBY = TX // BX, TY // BY
    EX = TX + 2 * HX
    EG = EX // PK
    G = TX // PK
    OX = slice(HX, HX + TX)
    OY = slice(HY, HY + TY)
    OP = slice(EX + XG, EX + XG + G)

    at = {a: lax.axis_index(a) for a in shape}
    up = {a: at[a] < shape[a] - 1 for a in shape}
    dn = {a: at[a] > 0 for a in shape}

    sends = []
    count = [0]

    class Copy:
        def __init__(self, src, dst, axis, way, also=None):
            i = count[0]
            count[0] += 1
            to = at[axis] + way
            self.desc = pltpu.make_async_remote_copy(
                src_ref=src, dst_ref=dst, send_sem=send.at[i], recv_sem=recv.at[i],
                device_id={axis: to}, device_id_type=MESH)
            self.out = up[axis] if way > 0 else dn[axis]
            self.into = dn[axis] if way > 0 else up[axis]
            if also is not None:
                self.out = jnp.logical_and(self.out, also)
                self.into = jnp.logical_and(self.into, also)
            sends.append(self)

        def start(self):
            @pl.when(self.out)
            def _():
                self.desc.start()
            return self

        def landed(self):
            @pl.when(self.into)
            def _():
                self.desc.wait_recv()

        def left(self):
            @pl.when(self.out)
            def _():
                self.desc.wait_send()

    lane = lax.broadcasted_iota(jnp.int32, (1, 1, LANES), 2)
    lane2 = lax.broadcasted_iota(jnp.int32, (1, LANES), 1)

    for ref in (E0, E1, YP, XP, ACC0, ACC1, BU, RZD, RZU, YRD, YRU, XPD, XPU, XMD, XMU,
                ZRD, ZRU, VE, YVD, YVU, VRD, VRU):
        ref[...] = jnp.zeros_like(ref)

    barrier = pltpu.get_barrier_semaphore()
    total = jnp.int32(0)
    for a in shape:
        for way, has in ((1, up[a]), (-1, dn[a])):
            @pl.when(has)
            def _(a=a, way=way):
                pl.semaphore_signal(barrier, inc=1, device_id={a: at[a] + way}, device_id_type=MESH)
            total = total + has.astype(jnp.int32)
    pl.semaphore_wait(barrier, total)

    def pack_own(E):
        for g in range(G):
            row = None
            for j in range(PK):
                turned = pltpu.roll(E[HX + PK * g + j, OY, :], (WIDE * j + HZ) % LANES, 1)
                row = turned if row is None else jnp.where(lane2 // WIDE == j, turned, row)
            S_of(E)[g] = row

    def S_of(E):
        return S.at[0] if E is E0 else S.at[1]

    def forward_exchange(E, k, between):
        s, rd, ru = S.at[k], RZD.at[k], RZU.at[k]
        zu = Copy(s, rd, "gz", 1).start()
        zd = Copy(s, ru, "gz", -1).start()
        lo_x, hi_x = slice(0, HX), slice(HX + TX, EX)
        xmu = Copy(E.at[TX:TX + HX, OY, :], E.at[lo_x, OY, :], "gx", 1).start()
        xmd = Copy(E.at[HX:2 * HX, OY, :], E.at[hi_x, OY, :], "gx", -1).start()
        top, bottom = slice(TY, TY + HY), slice(HY, 2 * HY)
        below, above = slice(0, HY), slice(HY + TY, 2 * HY + TY)

        def to_y(layers, also=None):
            return [Copy(E.at[layers, top, :], E.at[layers, below, :], "gy", 1, also).start(),
                    Copy(E.at[layers, bottom, :], E.at[layers, above, :], "gy", -1, also).start()]

        ys = to_y(OX)
        between()
        zu.landed()
        zd.landed()
        E[OP, OY, :] = jnp.where(lane % WIDE < HZ, rd[...], ru[...])
        first_p, last_p = slice(EX + XG, EX + 2 * XG), slice(EX + G, EX + G + XG)
        lo_p, hi_p = slice(EX, EX + XG), slice(EX + XG + G, EX + EG)
        xpu = Copy(E.at[last_p, OY, :], E.at[lo_p, OY, :], "gx", 1).start()
        xpd = Copy(E.at[first_p, OY, :], E.at[hi_p, OY, :], "gx", -1).start()
        ys += to_y(OP)
        xmu.landed()
        ys += to_y(lo_x, dn["gx"])
        xmd.landed()
        ys += to_y(hi_x, up["gx"])
        xpu.landed()
        ys += to_y(lo_p, dn["gx"])
        xpd.landed()
        ys += to_y(hi_p, up["gx"])
        for y in ys:
            y.landed()

    def unpack(E):
        for g in range(EG):
            row = E[EX + g]
            for j in range(PK):
                U[PK * g + j] = pltpu.roll(row, (LANES - (WIDE * j + HZ)) % LANES, 1)

    def taps(k, d, bx, by):
        e = frac[k, d, bx, by, 0].astype(jnp.float32) * 0.125
        e2 = e * e
        e3 = e2 * e
        return (0.5 * (2.0 * e2 - e3 - e), 0.5 * (3.0 * e3 - 5.0 * e2 + 2.0),
                0.5 * (4.0 * e2 - 3.0 * e3 + e), 0.5 * (e3 - e2))

    def gather_block(E, k, bx, by):
        a, b, c = shx[k, bx, by, 0], shy[k, bx, by, 0], shz[k, bx, by, 0]
        wx, wy, wz = (taps(k, d, bx, by) for d in range(3))
        y0 = by * BY if isinstance(by, int) else pl.multiple_of(by * BY, BY)
        x0 = bx * BX + (a + HX - 1)
        for i, ref in enumerate((E, U)):
            win = ref[pl.ds(x0, BX + 3), pl.ds(y0, WY), :]
            T[i * BX:(i + 1) * BX] = sum(wx[u] * win[u:u + BX] for u in range(4))
        y = sum(wy[v] * T[:, pl.ds(b + (HY - 1 + v), BY), :] for v in range(4))
        own, rim = y[:BX].reshape(BX * BY, LANES), y[BX:].reshape(BX * BY, LANES)
        res = None
        for w in range(4):
            s = c + (w - 1)
            inside = jnp.logical_and(lane2 >= s, lane2 < LANES + s)
            term = wz[w] * pltpu.roll(jnp.where(inside, own, rim), lax.rem(LANES - s, LANES), 1)
            res = term if res is None else res + term
        return res.reshape(BX, BY, LANES)

    def spread_block(ACC, vals, k, bx, by):
        a, b, c = shx[k, bx, by, 0], shy[k, bx, by, 0], shz[k, bx, by, 0]
        wx, wy, wz = (taps(k, d, bx, by) for d in range(3))
        flat = vals.reshape(BX * BY, LANES)
        own = rim = None
        for w in range(4):
            s = c + (w - 1)
            inside = jnp.logical_and(lane2 >= s, lane2 < LANES + s)
            term = wz[w] * pltpu.roll(flat, lax.rem(LANES + s, LANES), 1)
            o, r = jnp.where(inside, term, 0.0), jnp.where(inside, 0.0, term)
            own, rim = (o, r) if own is None else (own + o, rim + r)
        YP[0:BX, 2 * HY:2 * HY + BY, :] = own.reshape(BX, BY, LANES)
        YP[BX:2 * BX, 2 * HY:2 * HY + BY, :] = rim.reshape(BX, BY, LANES)
        t = sum(wy[v] * YP[:, pl.ds((HY + 1 - v) - b, WY), :] for v in range(4))
        y0 = by * BY if isinstance(by, int) else pl.multiple_of(by * BY, BY)
        x0 = bx * BX
        for i, ref in enumerate((ACC, BU)):
            for m in range(BX + 3):
                XP[i, 2 * HX + m] = sum(wx[u] * t[i * BX + m - u] for u in range(4) if 0 <= m - u < BX)
            here = (pl.ds(x0, WX), pl.ds(y0, WY), slice(None))
            ref[here] = ref[here] + XP[i, pl.ds((HX + 1) - a, WX)]

    def pack_rims(ACC):
        for g in range(EG):
            ACC[EX + g] = sum(pltpu.roll(BU[PK * g + j], (WIDE * j + HZ) % LANES, 1) for j in range(PK))

    def return_exchange(ACC, k, between):
        yrd, yru = YRD.at[k], YRU.at[k]
        below, above = slice(0, HY), slice(HY + TY, 2 * HY + TY)
        top, bottom = slice(TY, TY + HY), slice(HY, 2 * HY)

        def to_y(layers, also=None):
            return (Copy(ACC.at[layers, above, :], yrd.at[layers], "gy", 1, also).start(),
                    Copy(ACC.at[layers, below, :], yru.at[layers], "gy", -1, also).start())

        def fold_y(copies, layers):
            copies[0].landed()
            copies[1].landed()
            ACC[layers, bottom, :] = ACC[layers, bottom, :] + yrd[layers]
            ACC[layers, top, :] = ACC[layers, top, :] + yru[layers]

        lo_p, hi_p = slice(EX, EX + XG), slice(EX + XG + G, EX + EG)
        lo_x, hi_x = slice(0, HX), slice(HX + TX, EX)
        ylp = to_y(lo_p, dn["gx"])
        yhp = to_y(hi_p, up["gx"])
        ylx = to_y(lo_x, dn["gx"])
        yhx = to_y(hi_x, up["gx"])
        yop = to_y(OP)
        yom = to_y(OX)
        between()
        fold_y(ylp, lo_p)
        xpd = Copy(ACC.at[lo_p, OY, :], XPU.at[k], "gx", -1).start()
        fold_y(yhp, hi_p)
        xpu = Copy(ACC.at[hi_p, OY, :], XPD.at[k], "gx", 1).start()
        fold_y(ylx, lo_x)
        xmd = Copy(ACC.at[lo_x, OY, :], XMU.at[k], "gx", -1).start()
        fold_y(yhx, hi_x)
        xmu = Copy(ACC.at[hi_x, OY, :], XMD.at[k], "gx", 1).start()
        fold_y(yop, OP)
        xpd.landed()
        xpu.landed()
        first_p, last_p = slice(EX + XG, EX + 2 * XG), slice(EX + G, EX + G + XG)
        ACC[first_p, OY, :] = ACC[first_p, OY, :] + XPD[k]
        ACC[last_p, OY, :] = ACC[last_p, OY, :] + XPU[k]
        ZS[k] = ACC[OP, OY, :]
        zu = Copy(ZS.at[k], ZRD.at[k], "gz", 1).start()
        zd = Copy(ZS.at[k], ZRU.at[k], "gz", -1).start()
        fold_y(yom, OX)
        xmd.landed()
        xmu.landed()
        ACC[HX:2 * HX, OY, :] = ACC[HX:2 * HX, OY, :] + XMD[k]
        ACC[TX:TX + HX, OY, :] = ACC[TX:TX + HX, OY, :] + XMU[k]
        zu.landed()
        zd.landed()
        rims = jnp.where(lane % WIDE >= HZ, ZRD[k], ZRU[k])
        edge = jnp.logical_or(lane2 < HZ, lane2 >= LANES - HZ)
        for g in range(G):
            for j in range(PK):
                x = PK * g + j
                turned = pltpu.roll(rims[g], (LANES - (WIDE * j + HZ)) % LANES, 1)
                ADJ[x] = ACC[HX + x, OY, :] + jnp.where(edge, turned, 0.0)

    def each_block(fn):
        def step(n, carry):
            fn(n // NBY, n % NBY)
            return carry
        lax.fori_loop(0, NBX * NBY, step, 0)

    g0 = sum(grad[0, c].astype(jnp.float32) * vel[c] for c in range(3))
    E0[OX, OY, :] = STEP_SIZE * g0
    pack_own(E0)

    def nothing():
        pass

    forward_exchange(E0, 0, nothing)

    faces = []

    def send_faces():
        VE[:, LH:LH + TX, OY, :] = vel[...]
        for c in range(3):
            for i in range(TX // 2):
                for h in range(2):
                    YSU[c, i, LH * h:LH * (h + 1), :] = vel[c, 2 * i + h, TY - LH:TY, :]
                    YSD[c, i, LH * h:LH * (h + 1), :] = vel[c, 2 * i + h, 0:LH, :]
            for g in range(TX // VPK):
                row = None
                for j in range(VPK):
                    turned = pltpu.roll(vel[c, VPK * g + j], (2 * LH * j + LH) % LANES, 1)
                    row = turned if row is None else jnp.where(lane2 // (2 * LH) == j, turned, row)
                SV[c, g] = row
        faces.extend([
            Copy(SV, VRD, "gz", 1).start(), Copy(SV, VRU, "gz", -1).start(),
            Copy(vel.at[:, TX - LH:TX], VE.at[:, 0:LH, OY, :], "gx", 1).start(),
            Copy(vel.at[:, 0:LH], VE.at[:, LH + TX:2 * LH + TX, OY, :], "gx", -1).start(),
            Copy(YSU, YVD, "gy", 1).start(), Copy(YSD, YVU, "gy", -1).start()])

    send_faces()
    unpack(E0)

    def first(bx, by):
        y0 = pl.multiple_of(by * BY, BY)
        ST[pl.ds(bx * BX, BX), pl.ds(y0, BY), :] = gather_block(E0, 0, bx, by)

    each_block(first)
    g1 = sum(grad[1, c].astype(jnp.float32) * vel[c] for c in range(3))
    E1[OX, OY, :] = ST[...] + STEP_SIZE * g1
    pack_own(E1)

    forward_exchange(E1, 1, nothing)
    unpack(E1)

    def second(bx, by):
        spread_block(ACC1, gather_block(E1, 1, bx, by), 1, bx, by)

    each_block(second)
    pack_rims(ACC1)

    def regular():
        for f in faces:
            f.landed()
        for c in range(3):
            for i in range(TX // 2):
                for h in range(2):
                    VE[c, LH + 2 * i + h, HY - LH:HY, :] = YVD[c, i, LH * h:LH * (h + 1), :]
                    VE[c, LH + 2 * i + h, HY + TY:HY + TY + LH, :] = YVU[c, i, LH * h:LH * (h + 1), :]
        rows = lax.broadcasted_iota(jnp.int32, (2 * LANES, LANES), 0)
        cols = lax.broadcasted_iota(jnp.int32, (2 * LANES, LANES), 1)
        r = rows - LANES
        place = jnp.where(rows < LANES, rows, jnp.where(r < LH, r + LANES, r - LANES))
        known = jnp.logical_or(rows < LANES, jnp.logical_or(r < LH, r >= LANES - LH))
        gap = jnp.abs(place - cols)
        band = jnp.zeros((2 * LANES, LANES), jnp.float32)
        for k in range(5):
            tap = (3.0 if k == 0 else 1.0) * LAPLACE_TAPS[k]
            band = jnp.where(jnp.logical_and(known, gap == k), tap, band)
        for c in range(3):
            rims = []
            for g in range(TX // VPK):
                row = jnp.where(lane2 % (2 * LH) < LH, VRD[c, g], VRU[c, g])
                for j in range(VPK):
                    rims.append(pltpu.roll(row, (LANES - (2 * LH * j + LH)) % LANES, 1))
            rim = jnp.concatenate(rims, axis=0)
            own = vel[c].reshape(TX * TY, LANES)
            res = jnp.dot(jnp.concatenate([own, rim], axis=1), band,
                          preferred_element_type=jnp.float32,
                          precision=lax.Precision.HIGHEST).reshape(TX, TY, LANES)
            for k in range(1, 5):
                res = res + LAPLACE_TAPS[k] * (
                    VE[c, LH + k:LH + k + TX, OY, :] + VE[c, LH - k:LH - k + TX, OY, :]
                    + VE[c, LH:LH + TX, HY + k:HY + k + TY, :]
                    + VE[c, LH:LH + TX, HY - k:HY - k + TY, :])
            out[c] = (-REG_WEIGHT) * res

    return_exchange(ACC1, 1, regular)

    def third(bx, by):
        y0 = pl.multiple_of(by * BY, BY)
        vals = ADJ[pl.ds(bx * BX, BX), pl.ds(y0, BY), :]
        spread_block(ACC0, vals, 0, bx, by)

    BU[...] = jnp.zeros_like(BU)
    each_block(third)
    pack_rims(ACC0)

    def add_gauss(k):
        for c in range(3):
            out[c] = out[c] + STEP_SIZE * grad[k, c].astype(jnp.float32) * ADJ[...]

    return_exchange(ACC0, 0, functools.partial(add_gauss, 1))
    add_gauss(0)
    for copy in sends:
        copy.left()


COPIES = 18 * 2 + 18 * 2 + 6


def body(shape, velocity, gradients, shift_x, shift_y, shift_z, fractions):
    TX, TY, TZ = velocity.shape[1:]
    assert TZ == BZ == LANES and TX % VPK == 0 and TX % BX == 0 and TY % BY == 0
    EX, EY = TX + 2 * HX, TY + 2 * HY
    EG, G = EX // PK, TX // PK
    vm = lambda *s: pltpu.VMEM(s, jnp.float32)
    vmem = pl.BlockSpec(memory_space=pltpu.VMEM)
    smem = pl.BlockSpec(memory_space=pltpu.SMEM)
    return pl.pallas_call(
        functools.partial(kernel, shape),
        out_shape=jax.ShapeDtypeStruct(velocity.shape, jnp.float32),
        in_specs=[vmem, vmem, smem, smem, smem, smem],
        out_specs=vmem,
        scratch_shapes=[
            vm(EX + EG, EY, LANES), vm(EX + EG, EY, LANES),
            vm(EX, EY, LANES), vm(2 * BX, WY, LANES),
            vm(2 * BX, 2 * WY - BY, LANES), vm(2, 2 * WX - BX, WY, LANES),
            vm(EX + EG, EY, LANES), vm(EX + EG, EY, LANES),
            vm(EX, EY, LANES), vm(TX, TY, LANES), vm(TX, TY, LANES),
            vm(2, G, TY, LANES), vm(2, G, TY, LANES), vm(2, G, TY, LANES),
            vm(2, EX + EG, HY, LANES), vm(2, EX + EG, HY, LANES),
            vm(2, XG, TY, LANES), vm(2, XG, TY, LANES),
            vm(2, HX, TY, LANES), vm(2, HX, TY, LANES),
            vm(2, G, TY, LANES), vm(2, G, TY, LANES), vm(2, G, TY, LANES),
            vm(3, TX + 2 * LH, EY, LANES),
            vm(3, TX // 2, 2 * LH, LANES), vm(3, TX // 2, 2 * LH, LANES),
            vm(3, TX // 2, 2 * LH, LANES), vm(3, TX // 2, 2 * LH, LANES),
            vm(3, TX // VPK, TY, LANES), vm(3, TX // VPK, TY, LANES), vm(3, TX // VPK, TY, LANES),
            pltpu.SemaphoreType.DMA((COPIES,)), pltpu.SemaphoreType.DMA((COPIES,)),
        ],
        compiler_params=pltpu.CompilerParams(collective_id=0, has_side_effects=True),
    )(velocity, gradients, shift_x, shift_y, shift_z, fractions)


def solution(mesh):
    in_specs = (
        P(None, "gx", "gy", "gz"),
        P(None, None, "gx", "gy", "gz"),
        P(None, "gx", "gy", "gz"),
        P(None, "gx", "gy", "gz"),
        P(None, "gx", "gy", "gz"),
        P(None, None, "gx", "gy", "gz"),
    )
    out_specs = P(None, "gx", "gy", "gz")
    return jax.shard_map(functools.partial(body, dict(mesh.shape)), mesh=mesh, in_specs=in_specs,
                         out_specs=out_specs, check_vma=False)
```

```python
import functools

import jax
import jax.numpy as jnp
from jax import lax
from jax.experimental import pallas as pl
from jax.experimental.pallas import tpu as pltpu
from jax.sharding import PartitionSpec as P

BX = 8
BY = 8
BZ = 128
RX = 6
RY = 6
RZ = 14
STEPS = 2

STEP_SIZE = 0.5
REG_WEIGHT = 0.1
LAPLACE_TAPS = (-205.0 / 72.0, 8.0 / 5.0, -1.0 / 5.0, 8.0 / 315.0, -1.0 / 560.0)

HX = RX + 2
HY = RY + 2
HZ = RZ + 2
LANES = 128
PK = LANES // HZ
XG = HX // PK
LH = 4
VPK = LANES // (2 * LH)
WX = BX + 2 * HX
WY = BY + 2 * HY
MESH = pl.DeviceIdType.MESH
AXES = ("gx", "gy", "gz")
WAYS = sorted(((i, j, k) for i in (-1, 0, 1) for j in (-1, 0, 1) for k in (-1, 0, 1) if (i, j, k) != (0, 0, 0)),
              key=lambda d: -sum(map(abs, d)))


def piece(way, own, halo):
    return {-1: (0, halo), 0: (halo, halo + own), 1: (halo + own, 2 * halo + own)}[way]


def border(way, own, halo):
    return {-1: (halo, 2 * halo), 0: (halo, halo + own), 1: (own, halo + own)}[way]


def kernel(shape, vel, grad, shx, shy, shz, frac, out,
           E0, E1, U, T, YP, XP, ACC0, ACC1, BU, ST, ADJ, SP, SUM,
           VE, YSU, YSD, YVD, YVU, SV, VRD, VRU, *rest):
    back, (send, recv) = rest[:-2], rest[-2:]
    TX, TY, TZ = vel.shape[1:]
    NBX, NBY = TX // BX, TY // BY
    EX = TX + 2 * HX
    EG = EX // PK
    G = TX // PK
    OX = slice(HX, HX + TX)
    OY = slice(HY, HY + TY)

    at = {a: lax.axis_index(a) for a in AXES}

    def has(way):
        ok = None
        for a, w in zip(AXES, way):
            if w:
                one = at[a] < shape[a] - 1 if w > 0 else at[a] > 0
                ok = one if ok is None else jnp.logical_and(ok, one)
        return ok

    def device(way):
        return {a: at[a] + w for a, w in zip(AXES, way) if w}

    sends = []

    class Copy:
        def __init__(self, src, dst, way):
            i = len(sends)
            self.desc = pltpu.make_async_remote_copy(
                src_ref=src, dst_ref=dst, send_sem=send.at[i], recv_sem=recv.at[i],
                device_id=device(way), device_id_type=MESH)
            self.out, self.into = has(way), has(tuple(-w for w in way))
            sends.append(self)

        def start(self):
            pl.when(self.out)(self.desc.start)
            return self

        def landed(self):
            pl.when(self.into)(self.desc.wait_recv)

        def left(self):
            pl.when(self.out)(self.desc.wait_send)

    lane = lax.broadcasted_iota(jnp.int32, (1, 1, LANES), 2)
    lane2 = lax.broadcasted_iota(jnp.int32, (1, LANES), 1)

    for ref in (E0, E1, VE, YVD, YVU, VRD, VRU) + tuple(back):
        ref[...] = jnp.zeros_like(ref)

    barrier = pltpu.get_barrier_semaphore()
    total = jnp.int32(0)
    for way in WAYS:
        @pl.when(has(way))
        def _(way=way):
            pl.semaphore_signal(barrier, inc=1, device_id=device(way), device_id_type=MESH)
        total = total + has(way).astype(jnp.int32)

    def pack_own(E, k):
        for g in range(G):
            for side in range(2):
                row = None
                for j in range(PK):
                    turned = pltpu.roll(E[HX + PK * g + j, OY, :], (HZ * j + HZ * side) % LANES, 1)
                    row = turned if row is None else jnp.where(lane2 // HZ == j, turned, row)
                SP[k, side, HX // PK + g, OY, :] = row

    def region(way, dim_of):
        (x0, x1) = dim_of(way[0], G if way[2] else TX, XG if way[2] else HX)
        (y0, y1) = dim_of(way[1], TY, HY)
        return slice(x0, x1), slice(y0, y1)

    def rim(ref, way, where):
        xs, ys = where
        base = {0: 0, -1: EX, 1: EX + EG}[way]
        return ref.at[slice(base + xs.start, base + xs.stop), ys, :]

    def forward_exchange(E, k, between):
        copies = []
        for way in WAYS:
            xs, ys = region(way, border)
            if way[2]:
                src = SP.at[k, 0 if way[2] < 0 else 1, xs, ys, :]
            else:
                src = E.at[xs, ys, :]
            other = tuple(-w for w in way)
            copies.append(Copy(src, rim(E, other[2], region(other, piece)), way).start())
        between()
        for copy in copies:
            copy.landed()

    def unpack(E):
        for g in range(EG):
            below, above = E[EX + g], E[EX + EG + g]
            for j in range(PK):
                U[PK * g + j] = jnp.where(
                    lane2 < HZ, pltpu.roll(above, (LANES - HZ * j) % LANES, 1),
                    pltpu.roll(below, (LANES - HZ - HZ * j) % LANES, 1))

    def taps(k, d, bx, by):
        e = frac[k, bx, by, 0, d].astype(jnp.float32) * 0.125
        e2 = e * e
        e3 = e2 * e
        return (0.5 * (2.0 * e2 - e3 - e), 0.5 * (3.0 * e3 - 5.0 * e2 + 2.0),
                0.5 * (4.0 * e2 - 3.0 * e3 + e), 0.5 * (e3 - e2))

    def gather_block(E, k, bx, by):
        a, b, c = shx[k, bx, 0, by], shy[k, bx, 0, by], shz[k, bx, 0, by]
        wx, wy, wz = (taps(k, d, bx, by) for d in range(3))
        y0 = by * BY if isinstance(by, int) else pl.multiple_of(by * BY, BY)
        x0 = bx * BX + (a + HX - 1)
        for i, ref in enumerate((E, U)):
            win = ref[pl.ds(x0, BX + 3), pl.ds(y0, WY), :]
            T[i * BX:(i + 1) * BX] = sum(wx[u] * win[u:u + BX] for u in range(4))
        y = sum(wy[v] * T[:, pl.ds(b + (HY - 1 + v), BY), :] for v in range(4))
        own, rim = y[:BX].reshape(BX * BY, LANES), y[BX:].reshape(BX * BY, LANES)
        res = None
        for w in range(4):
            s = c + (w - 1)
            inside = jnp.logical_and(lane2 >= s, lane2 < LANES + s)
            term = wz[w] * pltpu.roll(jnp.where(inside, own, rim), lax.rem(LANES - s, LANES), 1)
            res = term if res is None else res + term
        return res.reshape(BX, BY, LANES)

    def spread_block(ACC, vals, k, bx, by):
        a, b, c = shx[k, bx, 0, by], shy[k, bx, 0, by], shz[k, bx, 0, by]
        wx, wy, wz = (taps(k, d, bx, by) for d in range(3))
        flat = vals.reshape(BX * BY, LANES)
        own = rim = None
        for w in range(4):
            s = c + (w - 1)
            inside = jnp.logical_and(lane2 >= s, lane2 < LANES + s)
            term = wz[w] * pltpu.roll(flat, lax.rem(LANES + s, LANES), 1)
            o, r = jnp.where(inside, term, 0.0), jnp.where(inside, 0.0, term)
            own, rim = (o, r) if own is None else (own + o, rim + r)
        YP[0:BX, 2 * HY:2 * HY + BY, :] = own.reshape(BX, BY, LANES)
        YP[BX:2 * BX, 2 * HY:2 * HY + BY, :] = rim.reshape(BX, BY, LANES)
        t = sum(wy[v] * YP[:, pl.ds((HY + 1 - v) - b, WY), :] for v in range(4))
        y0 = by * BY if isinstance(by, int) else pl.multiple_of(by * BY, BY)
        x0 = bx * BX
        for i, ref in enumerate((ACC, BU)):
            for m in range(BX + 3):
                XP[i, 2 * HX + m] = sum(wx[u] * t[i * BX + m - u] for u in range(4) if 0 <= m - u < BX)
            here = (pl.ds(x0, WX), pl.ds(y0, WY), slice(None))
            ref[here] = ref[here] + XP[i, pl.ds((HX + 1) - a, WX)]

    def pack_rims(ACC):
        for g in range(EG):
            for side in range(2):
                row = None
                for j in range(PK):
                    turned = pltpu.roll(BU[PK * g + j], (HZ * j + HZ * side) % LANES, 1)
                    row = turned if row is None else jnp.where(lane2 // HZ == j, turned, row)
                ACC[(EX + EG if side == 0 else EX) + g] = row

    def return_exchange(ACC, k, between):
        copies = []
        for n, way in enumerate(WAYS):
            copies.append((way, back[n].at[k], Copy(
                rim(ACC, way[2], region(way, piece)), back[n].at[k], way).start()))
        between()
        SUM[...] = jnp.zeros_like(SUM)
        for way, came, copy in copies:
            copy.landed()
            other = tuple(-w for w in way)
            xs, ys = region(other, border)
            if way[2]:
                side = 0 if way[2] > 0 else 1
                SUM[side, xs, ys, :] = SUM[side, xs, ys, :] + came[...]
            else:
                ACC[xs, ys, :] = ACC[xs, ys, :] + came[...]
        for g in range(G):
            first, last = SUM[0, XG + g, OY, :], SUM[1, XG + g, OY, :]
            for j in range(PK):
                x = PK * g + j
                turned = jnp.where(lane2 < HZ, pltpu.roll(first, (LANES - HZ * j) % LANES, 1),
                                   pltpu.roll(last, (LANES - HZ - HZ * j) % LANES, 1))
                edge = jnp.logical_or(lane2 < HZ, lane2 >= LANES - HZ)
                ADJ[x] = ACC[HX + x, OY, :] + jnp.where(edge, turned, 0.0)

    def each_block(fn):
        def step(n, carry):
            fn(n // NBY, n % NBY)
            return carry
        lax.fori_loop(0, NBX * NBY, step, 0)

    E0[OX, OY, :] = STEP_SIZE * sum(grad[0, c].astype(jnp.float32) * vel[c] for c in range(3))
    pack_own(E0, 0)
    pl.semaphore_wait(barrier, total)

    def prepare():
        for ref in (YP, XP, ACC0, ACC1, BU):
            ref[...] = jnp.zeros_like(ref)
        send_faces()

    def nothing():
        pass

    faces = []

    def send_faces():
        VE[:, LH:LH + TX, OY, :] = vel[...]
        for c in range(3):
            for i in range(TX // 2):
                for h in range(2):
                    YSU[c, i, LH * h:LH * (h + 1), :] = vel[c, 2 * i + h, TY - LH:TY, :]
                    YSD[c, i, LH * h:LH * (h + 1), :] = vel[c, 2 * i + h, 0:LH, :]
            for g in range(TX // VPK):
                row = None
                for j in range(VPK):
                    turned = pltpu.roll(vel[c, VPK * g + j], (2 * LH * j + LH) % LANES, 1)
                    row = turned if row is None else jnp.where(lane2 // (2 * LH) == j, turned, row)
                SV[c, g] = row
        faces.extend([
            Copy(SV, VRD, (0, 0, 1)).start(), Copy(SV, VRU, (0, 0, -1)).start(),
            Copy(vel.at[:, TX - LH:TX], VE.at[:, 0:LH, OY, :], (1, 0, 0)).start(),
            Copy(vel.at[:, 0:LH], VE.at[:, LH + TX:2 * LH + TX, OY, :], (-1, 0, 0)).start(),
            Copy(YSU, YVD, (0, 1, 0)).start(), Copy(YSD, YVU, (0, -1, 0)).start()])

    forward_exchange(E0, 0, prepare)
    unpack(E0)

    def first(bx, by):
        y0 = pl.multiple_of(by * BY, BY)
        ST[pl.ds(bx * BX, BX), pl.ds(y0, BY), :] = gather_block(E0, 0, bx, by)

    each_block(first)
    g1 = sum(grad[1, c].astype(jnp.float32) * vel[c] for c in range(3))
    E1[OX, OY, :] = ST[...] + STEP_SIZE * g1
    pack_own(E1, 1)

    forward_exchange(E1, 1, nothing)
    unpack(E1)

    def second(bx, by):
        spread_block(ACC1, gather_block(E1, 1, bx, by), 1, bx, by)

    each_block(second)
    pack_rims(ACC1)

    def regular():
        for f in faces:
            f.landed()
        for c in range(3):
            for i in range(TX // 2):
                for h in range(2):
                    VE[c, LH + 2 * i + h, HY - LH:HY, :] = YVD[c, i, LH * h:LH * (h + 1), :]
                    VE[c, LH + 2 * i + h, HY + TY:HY + TY + LH, :] = YVU[c, i, LH * h:LH * (h + 1), :]
        rows = lax.broadcasted_iota(jnp.int32, (2 * LANES, LANES), 0)
        cols = lax.broadcasted_iota(jnp.int32, (2 * LANES, LANES), 1)
        r = rows - LANES
        place = jnp.where(rows < LANES, rows, jnp.where(r < LH, r + LANES, r - LANES))
        known = jnp.logical_or(rows < LANES, jnp.logical_or(r < LH, r >= LANES - LH))
        gap = jnp.abs(place - cols)
        band = jnp.zeros((2 * LANES, LANES), jnp.float32)
        for k in range(5):
            tap = (3.0 if k == 0 else 1.0) * LAPLACE_TAPS[k]
            band = jnp.where(jnp.logical_and(known, gap == k), tap, band)
        for c in range(3):
            rims = []
            for g in range(TX // VPK):
                row = jnp.where(lane2 % (2 * LH) < LH, VRD[c, g], VRU[c, g])
                for j in range(VPK):
                    rims.append(pltpu.roll(row, (LANES - (2 * LH * j + LH)) % LANES, 1))
            rim = jnp.concatenate(rims, axis=0)
            own = vel[c].reshape(TX * TY, LANES)
            res = jnp.dot(jnp.concatenate([own, rim], axis=1), band,
                          preferred_element_type=jnp.float32,
                          precision=lax.Precision.HIGHEST).reshape(TX, TY, LANES)
            for k in range(1, 5):
                res = res + LAPLACE_TAPS[k] * (
                    VE[c, LH + k:LH + k + TX, OY, :] + VE[c, LH - k:LH - k + TX, OY, :]
                    + VE[c, LH:LH + TX, HY + k:HY + k + TY, :]
                    + VE[c, LH:LH + TX, HY - k:HY - k + TY, :])
            out[c] = (-REG_WEIGHT) * res

    return_exchange(ACC1, 1, regular)

    def third(bx, by):
        y0 = pl.multiple_of(by * BY, BY)
        vals = ADJ[pl.ds(bx * BX, BX), pl.ds(y0, BY), :]
        spread_block(ACC0, vals, 0, bx, by)

    BU[...] = jnp.zeros_like(BU)
    each_block(third)
    pack_rims(ACC0)

    def add_gauss(k):
        for c in range(3):
            out[c] = out[c] + STEP_SIZE * grad[k, c].astype(jnp.float32) * ADJ[...]

    return_exchange(ACC0, 0, functools.partial(add_gauss, 1))
    add_gauss(0)
    for copy in sends:
        copy.left()


COPIES = 4 * len(WAYS) + 6


def body(shape, velocity, gradients, shift_x, shift_y, shift_z, fractions):
    TX, TY, TZ = velocity.shape[1:]
    assert TZ == BZ == LANES and TX % VPK == 0 and TX % BX == 0 and TY % BY == 0
    EX, EY = TX + 2 * HX, TY + 2 * HY
    EG, G = EX // PK, TX // PK

    def span(way):
        groups = (XG if way[0] else G) if way[2] else (HX if way[0] else TX)
        return groups, HY if way[1] else TY

    vm = lambda *s: pltpu.VMEM(s, jnp.float32)
    vmem = pl.BlockSpec(memory_space=pltpu.VMEM)
    smem = pl.BlockSpec(memory_space=pltpu.SMEM)
    shift_x, shift_y, shift_z = (s.transpose(0, 1, 3, 2) for s in (shift_x, shift_y, shift_z))
    fractions = fractions.transpose(0, 2, 3, 4, 1)
    return pl.pallas_call(
        functools.partial(kernel, shape),
        out_shape=jax.ShapeDtypeStruct(velocity.shape, jnp.float32),
        in_specs=[vmem, vmem, smem, smem, smem, smem],
        out_specs=vmem,
        scratch_shapes=[
            vm(EX + 2 * EG, EY, LANES), vm(EX + 2 * EG, EY, LANES),
            vm(EX, EY, LANES), vm(2 * BX, WY, LANES),
            vm(2 * BX, 2 * WY - BY, LANES), vm(2, 2 * WX - BX, WY, LANES),
            vm(EX + 2 * EG, EY, LANES), vm(EX + 2 * EG, EY, LANES),
            vm(EX, EY, LANES), vm(TX, TY, LANES), vm(TX, TY, LANES),
            vm(2, 2, EG, EY, LANES), vm(2, EG, EY, LANES),
            vm(3, TX + 2 * LH, EY, LANES),
            vm(3, TX // 2, 2 * LH, LANES), vm(3, TX // 2, 2 * LH, LANES),
            vm(3, TX // 2, 2 * LH, LANES), vm(3, TX // 2, 2 * LH, LANES),
            vm(3, TX // VPK, TY, LANES), vm(3, TX // VPK, TY, LANES), vm(3, TX // VPK, TY, LANES),
            *[vm(2, *span(way), LANES) for way in WAYS],
            pltpu.SemaphoreType.DMA((COPIES,)), pltpu.SemaphoreType.DMA((COPIES,)),
        ],
        compiler_params=pltpu.CompilerParams(collective_id=0, has_side_effects=True,
                                             vmem_limit_bytes=16 << 20),
    )(velocity, gradients, shift_x, shift_y, shift_z, fractions)


def solution(mesh):
    in_specs = (
        P(None, "gx", "gy", "gz"),
        P(None, None, "gx", "gy", "gz"),
        P(None, "gx", "gy", "gz"),
        P(None, "gx", "gy", "gz"),
        P(None, "gx", "gy", "gz"),
        P(None, None, "gx", "gy", "gz"),
    )
    out_specs = P(None, "gx", "gy", "gz")
    return jax.shard_map(functools.partial(body, dict(mesh.shape)), mesh=mesh, in_specs=in_specs,
                         out_specs=out_specs, check_vma=False)
```

```python
import functools

import jax
import jax.numpy as jnp
from jax import lax
from jax.experimental import pallas as pl
from jax.experimental.pallas import tpu as pltpu
from jax.sharding import PartitionSpec as P

BX = 8
BY = 8
BZ = 128
RX = 6
RY = 6
RZ = 14
STEPS = 2

STEP_SIZE = 0.5
REG_WEIGHT = 0.1
LAPLACE_TAPS = (-205.0 / 72.0, 8.0 / 5.0, -1.0 / 5.0, 8.0 / 315.0, -1.0 / 560.0)

HX = RX + 2
HY = RY + 2
HZ = RZ + 2
LANES = 128
PK = LANES // HZ
XG = HX // PK
LH = 4
VPK = LANES // (2 * LH)
WX = BX + 2 * HX
WY = BY + 2 * HY
MESH = pl.DeviceIdType.MESH
AXES = ("gx", "gy", "gz")
WAYS = sorted(((i, j, k) for i in (-1, 0, 1) for j in (-1, 0, 1) for k in (-1, 0, 1) if (i, j, k) != (0, 0, 0)),
              key=lambda d: -sum(map(abs, d)))


def piece(way, own, halo):
    return {-1: (0, halo), 0: (halo, halo + own), 1: (halo + own, 2 * halo + own)}[way]


def border(way, own, halo):
    return {-1: (halo, 2 * halo), 0: (halo, halo + own), 1: (own, halo + own)}[way]


def kernel(shape, vel_in, grad_in, shx_in, shy_in, shz_in, frac_in, out,
           vel, grad, shx, shy, shz, frac, arrive,
           E0, E1, U, YP, XP, ACC0, ACC1, T, ST, ADJ, SP, SUM,
           VE, YSU, YSD, YVD, YVU, SV, VRD, VRU, *rest):
    back, (send, recv) = rest[:-2], rest[-2:]
    TX, TY, TZ = vel.shape[1:]
    NBX, NBY = TX // BX, TY // BY
    EX = TX + 2 * HX
    EG = EX // PK
    G = TX // PK
    OX = slice(HX, HX + TX)
    OY = slice(HY, HY + TY)

    at = {a: lax.axis_index(a) for a in AXES}

    def has(way):
        ok = None
        for a, w in zip(AXES, way):
            if w:
                one = at[a] < shape[a] - 1 if w > 0 else at[a] > 0
                ok = one if ok is None else jnp.logical_and(ok, one)
        return ok

    def device(way):
        return {a: at[a] + w for a, w in zip(AXES, way) if w}

    loads = [pltpu.make_async_copy(a, b, arrive.at[n]) for n, (a, b) in enumerate((
        (vel_in, vel), (grad_in, grad), (shx_in, shx), (shy_in, shy), (shz_in, shz), (frac_in, frac)))]
    for load in loads:
        load.start()

    sends = []

    class Copy:
        def __init__(self, src, dst, way):
            i = len(sends)
            self.desc = pltpu.make_async_remote_copy(
                src_ref=src, dst_ref=dst, send_sem=send.at[i], recv_sem=recv.at[i],
                device_id=device(way), device_id_type=MESH)
            self.out, self.into = has(way), has(tuple(-w for w in way))
            sends.append(self)

        def start(self):
            pl.when(self.out)(self.desc.start)
            return self

        def landed(self):
            pl.when(self.into)(self.desc.wait_recv)

        def left(self):
            pl.when(self.out)(self.desc.wait_send)

    lane = lax.broadcasted_iota(jnp.int32, (1, 1, LANES), 2)
    lane2 = lax.broadcasted_iota(jnp.int32, (1, LANES), 1)

    for ref in (E0, E1, VE, YVD, YVU, VRD, VRU) + tuple(back):
        ref[...] = jnp.zeros_like(ref)

    barrier = pltpu.get_barrier_semaphore()
    total = jnp.int32(0)
    for way in WAYS:
        @pl.when(has(way))
        def _(way=way):
            pl.semaphore_signal(barrier, inc=1, device_id=device(way), device_id_type=MESH)
        total = total + has(way).astype(jnp.int32)

    group = lane2 // HZ

    def packed(layer, g):
        first = last = None
        for j in range(PK):
            turned = pltpu.roll(layer(PK * g + j), HZ * j, 1) if j else layer(PK * g)
            first = turned if j == 0 else jnp.where(group == j, turned, first)
            last = turned if j == 0 else jnp.where(group == j - 1, turned, last)
        return first, last

    def unpacked(first, last, j):
        both = jnp.where(group == j, first, last)
        return pltpu.roll(both, LANES - HZ * j, 1) if j else both

    def pack_own(E, k):
        def layer(x):
            return E[HX + x, OY, :]
        for g in range(G):
            SP[k, 0, XG + g, OY, :], SP[k, 1, XG + g, OY, :] = packed(layer, g)

    def region(way, dim_of):
        (x0, x1) = dim_of(way[0], G if way[2] else TX, XG if way[2] else HX)
        (y0, y1) = dim_of(way[1], TY, HY)
        return slice(x0, x1), slice(y0, y1)

    def rim(ref, way, where):
        xs, ys = where
        base = {0: 0, -1: EX, 1: EX + EG}[way]
        return ref.at[slice(base + xs.start, base + xs.stop), ys, :]

    def forward_exchange(E, k, between):
        copies = []
        for way in WAYS:
            xs, ys = region(way, border)
            if way[2]:
                src = SP.at[k, 0 if way[2] < 0 else 1, xs, ys, :]
            else:
                src = E.at[xs, ys, :]
            other = tuple(-w for w in way)
            copies.append(Copy(src, rim(E, other[2], region(other, piece)), way).start())
        between()
        for copy in copies:
            copy.landed()

    def unpack(E):
        for g in range(EG):
            below, above = E[EX + g], E[EX + EG + g]
            for j in range(PK):
                U[PK * g + j] = unpacked(above, below, j)

    def taps(k, d, bx, by):
        e = frac[k, bx, by, 0, d].astype(jnp.float32) * 0.125
        e2 = e * e
        e3 = e2 * e
        return (0.5 * (2.0 * e2 - e3 - e), 0.5 * (3.0 * e3 - 5.0 * e2 + 2.0),
                0.5 * (4.0 * e2 - 3.0 * e3 + e), 0.5 * (e3 - e2))

    def gather_block(E, k, bx, by):
        n = bx * NBY + by
        a, b, c = shx[k, bx, 0, by], shy[k, bx, 0, by], shz[k, bx, 0, by]
        wx, wy, wz = (taps(k, d, bx, by) for d in range(3))
        y0 = by * BY
        x0 = bx * BX + (a + HX - 1)
        for i, ref in enumerate((E, U)):
            win = ref[pl.ds(x0, BX + 3), pl.ds(y0, WY), :]
            T[n, i * BX:(i + 1) * BX] = sum(wx[u] * win[u:u + BX] for u in range(4))
        y = sum(wy[v] * T[n, :, pl.ds(b + (HY - 1 + v), BY), :] for v in range(4))
        own, rim = y[:BX].reshape(BX * BY, LANES), y[BX:].reshape(BX * BY, LANES)
        res = None
        for w in range(4):
            s = c + (w - 1)
            inside = jnp.logical_and(lane2 >= s, lane2 < LANES + s)
            term = wz[w] * pltpu.roll(jnp.where(inside, own, rim), lax.rem(LANES - s, LANES), 1)
            res = term if res is None else res + term
        return res.reshape(BX, BY, LANES)

    def spread_block(vals, k, bx, by):
        n = bx * NBY + by
        a, b, c = shx[k, bx, 0, by], shy[k, bx, 0, by], shz[k, bx, 0, by]
        wx, wy, wz = (taps(k, d, bx, by) for d in range(3))
        flat = vals.reshape(BX * BY, LANES)
        own = rim = None
        for w in range(4):
            s = c + (w - 1)
            inside = jnp.logical_and(lane2 >= s, lane2 < LANES + s)
            term = wz[w] * pltpu.roll(flat, lax.rem(LANES + s, LANES), 1)
            o, r = jnp.where(inside, term, 0.0), jnp.where(inside, 0.0, term)
            own, rim = (o, r) if own is None else (own + o, rim + r)
        YP[n, 0:BX, 2 * HY:2 * HY + BY, :] = own.reshape(BX, BY, LANES)
        YP[n, BX:2 * BX, 2 * HY:2 * HY + BY, :] = rim.reshape(BX, BY, LANES)
        t = sum(wy[v] * YP[n, :, pl.ds((HY + 1 - v) - b, WY), :] for v in range(4))
        for i in range(2):
            for m in range(BX + 3):
                XP[n, i, 2 * HX + m] = sum(wx[u] * t[i * BX + m - u] for u in range(4) if 0 <= m - u < BX)

    def collect(ACC, k):
        starts = {(bx, by): (HX + 1) - shx[k, bx, 0, by] for bx in range(NBX) for by in range(NBY)}

        def layer(i, x):
            tiles = [None] * ((TY + 2 * HY) // BY)
            for bx in range(NBX):
                if not 0 <= x - bx * BX < WX:
                    continue
                for by in range(NBY):
                    rows = XP[bx * NBY + by, i, starts[bx, by] + (x - bx * BX)]
                    for q in range(WY // BY):
                        part = rows[q * BY:(q + 1) * BY]
                        old = tiles[by + q]
                        tiles[by + q] = part if old is None else old + part
            return jnp.concatenate(tiles, axis=0)

        for g in range(EG):
            above, below = packed(functools.partial(layer, 1), g)
            ACC[EX + EG + g] = above
            ACC[EX + g] = below
        for x in range(EX):
            ACC[x] = layer(0, x)

    def return_exchange(ACC, k, between):
        copies = []
        for n, way in enumerate(WAYS):
            copies.append((way, back[n].at[k], Copy(
                rim(ACC, way[2], region(way, piece)), back[n].at[k], way).start()))
        between()
        SUM[...] = jnp.zeros_like(SUM)
        for way, came, copy in copies:
            copy.landed()
            other = tuple(-w for w in way)
            xs, ys = region(other, border)
            if way[2]:
                side = 0 if way[2] > 0 else 1
                SUM[side, xs, ys, :] = SUM[side, xs, ys, :] + came[...]
            else:
                ACC[xs, ys, :] = ACC[xs, ys, :] + came[...]
        for g in range(G):
            first, last = SUM[0, XG + g, OY, :], SUM[1, XG + g, OY, :]
            for j in range(PK):
                x = PK * g + j
                edge = jnp.logical_or(lane2 < HZ, lane2 >= LANES - HZ)
                ADJ[x] = ACC[HX + x, OY, :] + jnp.where(edge, unpacked(first, last, j), 0.0)

    def each_block(fn):
        for bx in range(NBX):
            for by in range(NBY):
                fn(bx, by)

    for load in loads:
        load.wait()
    E0[OX, OY, :] = STEP_SIZE * sum(grad[0, c].astype(jnp.float32) * vel[c] for c in range(3))
    pack_own(E0, 0)
    pl.semaphore_wait(barrier, total)

    def prepare():
        for ref in (YP, XP):
            ref[...] = jnp.zeros_like(ref)
        send_faces()

    def nothing():
        pass

    faces = []

    def send_faces():
        VE[:, LH:LH + TX, OY, :] = vel[...]
        for c in range(3):
            for i in range(TX // 2):
                for h in range(2):
                    YSU[c, i, LH * h:LH * (h + 1), :] = vel[c, 2 * i + h, TY - LH:TY, :]
                    YSD[c, i, LH * h:LH * (h + 1), :] = vel[c, 2 * i + h, 0:LH, :]
            for g in range(TX // VPK):
                row = None
                for j in range(VPK):
                    turned = pltpu.roll(vel[c, VPK * g + j], (2 * LH * j + LH) % LANES, 1)
                    row = turned if row is None else jnp.where(lane2 // (2 * LH) == j, turned, row)
                SV[c, g] = row
        faces.extend([
            Copy(SV, VRD, (0, 0, 1)).start(), Copy(SV, VRU, (0, 0, -1)).start(),
            Copy(vel.at[:, TX - LH:TX], VE.at[:, 0:LH, OY, :], (1, 0, 0)).start(),
            Copy(vel.at[:, 0:LH], VE.at[:, LH + TX:2 * LH + TX, OY, :], (-1, 0, 0)).start(),
            Copy(YSU, YVD, (0, 1, 0)).start(), Copy(YSD, YVU, (0, -1, 0)).start()])

    forward_exchange(E0, 0, prepare)
    unpack(E0)

    def first(bx, by):
        y0 = by * BY
        ST[pl.ds(bx * BX, BX), pl.ds(y0, BY), :] = gather_block(E0, 0, bx, by)

    each_block(first)
    g1 = sum(grad[1, c].astype(jnp.float32) * vel[c] for c in range(3))
    E1[OX, OY, :] = ST[...] + STEP_SIZE * g1
    pack_own(E1, 1)

    forward_exchange(E1, 1, nothing)
    unpack(E1)

    def second(bx, by):
        spread_block(gather_block(E1, 1, bx, by), 1, bx, by)

    each_block(second)
    collect(ACC1, 1)

    def regular():
        for f in faces:
            f.landed()
        for c in range(3):
            for i in range(TX // 2):
                for h in range(2):
                    VE[c, LH + 2 * i + h, HY - LH:HY, :] = YVD[c, i, LH * h:LH * (h + 1), :]
                    VE[c, LH + 2 * i + h, HY + TY:HY + TY + LH, :] = YVU[c, i, LH * h:LH * (h + 1), :]
        rows = lax.broadcasted_iota(jnp.int32, (2 * LANES, LANES), 0)
        cols = lax.broadcasted_iota(jnp.int32, (2 * LANES, LANES), 1)
        r = rows - LANES
        place = jnp.where(rows < LANES, rows, jnp.where(r < LH, r + LANES, r - LANES))
        known = jnp.logical_or(rows < LANES, jnp.logical_or(r < LH, r >= LANES - LH))
        gap = jnp.abs(place - cols)
        band = jnp.zeros((2 * LANES, LANES), jnp.float32)
        for k in range(5):
            tap = (3.0 if k == 0 else 1.0) * LAPLACE_TAPS[k]
            band = jnp.where(jnp.logical_and(known, gap == k), tap, band)
        for c in range(3):
            rims = []
            for g in range(TX // VPK):
                row = jnp.where(lane2 % (2 * LH) < LH, VRD[c, g], VRU[c, g])
                for j in range(VPK):
                    rims.append(pltpu.roll(row, (LANES - (2 * LH * j + LH)) % LANES, 1))
            rim = jnp.concatenate(rims, axis=0)
            own = vel[c].reshape(TX * TY, LANES)
            res = jnp.dot(jnp.concatenate([own, rim], axis=1), band,
                          preferred_element_type=jnp.float32,
                          precision=lax.Precision.HIGHEST).reshape(TX, TY, LANES)
            for k in range(1, 5):
                res = res + LAPLACE_TAPS[k] * (
                    VE[c, LH + k:LH + k + TX, OY, :] + VE[c, LH - k:LH - k + TX, OY, :]
                    + VE[c, LH:LH + TX, HY + k:HY + k + TY, :]
                    + VE[c, LH:LH + TX, HY - k:HY - k + TY, :])
            out[c] = (-REG_WEIGHT) * res

    return_exchange(ACC1, 1, regular)

    def third(bx, by):
        y0 = by * BY
        vals = ADJ[pl.ds(bx * BX, BX), pl.ds(y0, BY), :]
        spread_block(vals, 0, bx, by)

    each_block(third)
    collect(ACC0, 0)

    def add_gauss(k):
        for c in range(3):
            out[c] = out[c] + STEP_SIZE * grad[k, c].astype(jnp.float32) * ADJ[...]

    def last():
        add_gauss(1)
        for copy in sends:
            copy.left()

    return_exchange(ACC0, 0, last)
    add_gauss(0)


COPIES = 4 * len(WAYS) + 6


def body(shape, velocity, gradients, shift_x, shift_y, shift_z, fractions):
    TX, TY, TZ = velocity.shape[1:]
    assert TZ == BZ == LANES and TX % VPK == 0 and TX % BX == 0 and TY % BY == 0
    EX, EY = TX + 2 * HX, TY + 2 * HY
    EG, G = EX // PK, TX // PK
    NB = (TX // BX) * (TY // BY)

    def span(way):
        groups = (XG if way[0] else G) if way[2] else (HX if way[0] else TX)
        return groups, HY if way[1] else TY

    vm = lambda *s: pltpu.VMEM(s, jnp.float32)
    vmem = pl.BlockSpec(memory_space=pltpu.VMEM)
    hbm = pl.BlockSpec(memory_space=pltpu.HBM)
    shift_x, shift_y, shift_z = (s.transpose(0, 1, 3, 2) for s in (shift_x, shift_y, shift_z))
    fractions = fractions.transpose(0, 2, 3, 4, 1)
    return pl.pallas_call(
        functools.partial(kernel, shape),
        out_shape=jax.ShapeDtypeStruct(velocity.shape, jnp.float32),
        in_specs=[hbm] * 6,
        out_specs=vmem,
        scratch_shapes=[
            pltpu.VMEM(velocity.shape, velocity.dtype), pltpu.VMEM(gradients.shape, gradients.dtype),
            *[pltpu.SMEM(s.shape, s.dtype) for s in (shift_x, shift_y, shift_z, fractions)],
            pltpu.SemaphoreType.DMA((6,)),
            vm(EX + 2 * EG, EY, LANES), vm(EX + 2 * EG, EY, LANES),
            vm(EX, EY, LANES),
            vm(NB, 2 * BX, 2 * WY - BY, LANES), vm(NB, 2, 2 * WX - BX, WY, LANES),
            vm(EX + 2 * EG, EY, LANES), vm(EX + 2 * EG, EY, LANES),
            vm(NB, 2 * BX, WY, LANES), vm(TX, TY, LANES), vm(TX, TY, LANES),
            vm(2, 2, EG, EY, LANES), vm(2, EG, EY, LANES),
            vm(3, TX + 2 * LH, EY, LANES),
            vm(3, TX // 2, 2 * LH, LANES), vm(3, TX // 2, 2 * LH, LANES),
            vm(3, TX // 2, 2 * LH, LANES), vm(3, TX // 2, 2 * LH, LANES),
            vm(3, TX // VPK, TY, LANES), vm(3, TX // VPK, TY, LANES), vm(3, TX // VPK, TY, LANES),
            *[vm(2, *span(way), LANES) for way in WAYS],
            pltpu.SemaphoreType.DMA((COPIES,)), pltpu.SemaphoreType.DMA((COPIES,)),
        ],
        compiler_params=pltpu.CompilerParams(collective_id=0, has_side_effects=True,
                                             vmem_limit_bytes=60 * 1024 * 1024),
    )(velocity, gradients, shift_x, shift_y, shift_z, fractions)


def solution(mesh):
    in_specs = (
        P(None, "gx", "gy", "gz"),
        P(None, None, "gx", "gy", "gz"),
        P(None, "gx", "gy", "gz"),
        P(None, "gx", "gy", "gz"),
        P(None, "gx", "gy", "gz"),
        P(None, None, "gx", "gy", "gz"),
    )
    out_specs = P(None, "gx", "gy", "gz")
    return jax.shard_map(functools.partial(body, dict(mesh.shape)), mesh=mesh, in_specs=in_specs,
                         out_specs=out_specs, check_vma=False)
```

```python
import functools

import jax
import jax.numpy as jnp
from jax import lax
from jax.experimental import pallas as pl
from jax.experimental.pallas import tpu as pltpu
from jax.sharding import PartitionSpec as P

BX = 8
BY = 8
BZ = 128
RX = 6
RY = 6
RZ = 14
STEPS = 2

STEP_SIZE = 0.5
REG_WEIGHT = 0.1
LAPLACE_TAPS = (-205.0 / 72.0, 8.0 / 5.0, -1.0 / 5.0, 8.0 / 315.0, -1.0 / 560.0)

HX = RX + 2
HY = RY + 2
HZ = RZ + 2
LANES = 128
PK = LANES // HZ
XG = HX // PK
LH = 4
VPK = LANES // (2 * LH)
WX = BX + 2 * HX
WY = BY + 2 * HY
MESH = pl.DeviceIdType.MESH
AXES = ("gx", "gy", "gz")
WAYS = sorted(((i, j, k) for i in (-1, 0, 1) for j in (-1, 0, 1) for k in (-1, 0, 1) if (i, j, k) != (0, 0, 0)),
              key=lambda d: -sum(map(abs, d)))


def piece(way, own, halo):
    return {-1: (0, halo), 0: (halo, halo + own), 1: (halo + own, 2 * halo + own)}[way]


def border(way, own, halo):
    return {-1: (halo, 2 * halo), 0: (halo, halo + own), 1: (own, halo + own)}[way]


def kernel(shape, vel_in, grad_in, shx_in, shy_in, shz_in, frac_in, out,
           vel, grad, shx, shy, shz, frac, arrive,
           E0, E1, U, YP, XP, ACC0, ACC1, T, ST, ADJ, SP, SUM,
           VE, YSU, YSD, YVD, YVU, SV, VRD, VRU, *rest):
    back, (send, recv) = rest[:-2], rest[-2:]
    TX, TY, TZ = vel.shape[1:]
    NBX, NBY = TX // BX, TY // BY
    EX = TX + 2 * HX
    EG = EX // PK
    G = TX // PK
    OX = slice(HX, HX + TX)
    OY = slice(HY, HY + TY)

    at = {a: lax.axis_index(a) for a in AXES}

    def has(way):
        ok = None
        for a, w in zip(AXES, way):
            if w:
                one = at[a] < shape[a] - 1 if w > 0 else at[a] > 0
                ok = one if ok is None else jnp.logical_and(ok, one)
        return ok

    def device(way):
        return {a: at[a] + w for a, w in zip(AXES, way) if w}

    loads = [pltpu.make_async_copy(a, b, arrive.at[n]) for n, (a, b) in enumerate((
        (vel_in, vel), (grad_in, grad), (shx_in, shx), (shy_in, shy), (shz_in, shz), (frac_in, frac)))]
    for load in loads:
        load.start()

    sends = []

    class Copy:
        def __init__(self, src, dst, way):
            i = len(sends)
            self.desc = pltpu.make_async_remote_copy(
                src_ref=src, dst_ref=dst, send_sem=send.at[i], recv_sem=recv.at[i],
                device_id=device(way), device_id_type=MESH)
            self.out, self.into = has(way), has(tuple(-w for w in way))
            sends.append(self)

        def start(self):
            pl.when(self.out)(self.desc.start)
            return self

        def landed(self):
            pl.when(self.into)(self.desc.wait_recv)

        def left(self):
            pl.when(self.out)(self.desc.wait_send)

    lane = lax.broadcasted_iota(jnp.int32, (1, 1, LANES), 2)
    lane2 = lax.broadcasted_iota(jnp.int32, (1, LANES), 1)

    for ref in (E0, E1, VE, YVD, YVU, VRD, VRU) + tuple(back):
        ref[...] = jnp.zeros_like(ref)

    barrier = pltpu.get_barrier_semaphore()
    total = jnp.int32(0)
    for way in WAYS:
        @pl.when(has(way))
        def _(way=way):
            pl.semaphore_signal(barrier, inc=1, device_id=device(way), device_id_type=MESH)
        total = total + has(way).astype(jnp.int32)

    group = lane2 // HZ

    def packed(layer, g):
        first = last = None
        for j in range(PK):
            turned = pltpu.roll(layer(PK * g + j), HZ * j, 1) if j else layer(PK * g)
            first = turned if j == 0 else jnp.where(group == j, turned, first)
            last = turned if j == 0 else jnp.where(group == j - 1, turned, last)
        return first, last

    def unpacked(first, last, j):
        both = jnp.where(group == j, first, last)
        return pltpu.roll(both, LANES - HZ * j, 1) if j else both

    def pack_own(E, k):
        def layer(x):
            return E[HX + x, OY, :]
        for g in range(G):
            SP[k, 0, XG + g, OY, :], SP[k, 1, XG + g, OY, :] = packed(layer, g)

    def region(way, dim_of):
        (x0, x1) = dim_of(way[0], G if way[2] else TX, XG if way[2] else HX)
        (y0, y1) = dim_of(way[1], TY, HY)
        return slice(x0, x1), slice(y0, y1)

    def rim(ref, way, where):
        xs, ys = where
        base = {0: 0, -1: EX, 1: EX + EG}[way]
        return ref.at[slice(base + xs.start, base + xs.stop), ys, :]

    def forward_exchange(E, k, between):
        copies = []
        for way in WAYS:
            xs, ys = region(way, border)
            if way[2]:
                src = SP.at[k, 0 if way[2] < 0 else 1, xs, ys, :]
            else:
                src = E.at[xs, ys, :]
            other = tuple(-w for w in way)
            copies.append(Copy(src, rim(E, other[2], region(other, piece)), way).start())
        between()
        for copy in copies:
            copy.landed()

    def unpack(E):
        for g in range(EG):
            below, above = E[EX + g], E[EX + EG + g]
            for j in range(PK):
                U[PK * g + j] = unpacked(above, below, j)

    def taps(k, d, bx, by):
        e = frac[k, bx, by, 0, d].astype(jnp.float32) * 0.125
        e2 = e * e
        e3 = e2 * e
        return (0.5 * (2.0 * e2 - e3 - e), 0.5 * (3.0 * e3 - 5.0 * e2 + 2.0),
                0.5 * (4.0 * e2 - 3.0 * e3 + e), 0.5 * (e3 - e2))

    def gather_block(E, k, bx, by):
        n = bx * NBY + by
        a, b, c = shx[k, bx, 0, by], shy[k, bx, 0, by], shz[k, bx, 0, by]
        wx, wy, wz = (taps(k, d, bx, by) for d in range(3))
        y0 = by * BY
        x0 = bx * BX + (a + HX - 1)
        for i, ref in enumerate((E, U)):
            win = ref[pl.ds(x0, BX + 3), pl.ds(y0, WY), :]
            T[n, i * BX:(i + 1) * BX] = sum(wx[u] * win[u:u + BX] for u in range(4))
        y = sum(wy[v] * T[n, :, pl.ds(b + (HY - 1 + v), BY), :] for v in range(4))
        own, rim = y[:BX].reshape(BX * BY, LANES), y[BX:].reshape(BX * BY, LANES)
        res = None
        for w in range(4):
            s = c + (w - 1)
            inside = jnp.logical_and(lane2 >= s, lane2 < LANES + s)
            term = wz[w] * pltpu.roll(jnp.where(inside, own, rim), lax.rem(LANES - s, LANES), 1)
            res = term if res is None else res + term
        return res.reshape(BX, BY, LANES)

    def spread_block(vals, k, bx, by):
        n = bx * NBY + by
        a, b, c = shx[k, bx, 0, by], shy[k, bx, 0, by], shz[k, bx, 0, by]
        wx, wy, wz = (taps(k, d, bx, by) for d in range(3))
        flat = vals.reshape(BX * BY, LANES)
        own = rim = None
        for w in range(4):
            s = c + (w - 1)
            inside = jnp.logical_and(lane2 >= s, lane2 < LANES + s)
            term = wz[w] * pltpu.roll(flat, lax.rem(LANES + s, LANES), 1)
            o, r = jnp.where(inside, term, 0.0), jnp.where(inside, 0.0, term)
            own, rim = (o, r) if own is None else (own + o, rim + r)
        YP[n, 0:BX, 2 * HY:2 * HY + BY, :] = own.reshape(BX, BY, LANES)
        YP[n, BX:2 * BX, 2 * HY:2 * HY + BY, :] = rim.reshape(BX, BY, LANES)
        t = sum(wy[v] * YP[n, :, pl.ds((HY + 1 - v) - b, WY), :] for v in range(4))
        for i in range(2):
            for m in range(BX + 3):
                XP[n, i, 2 * HX + m] = sum(wx[u] * t[i * BX + m - u] for u in range(4) if 0 <= m - u < BX)

    def collect(ACC, k):
        starts = {(bx, by): (HX + 1) - shx[k, bx, 0, by] for bx in range(NBX) for by in range(NBY)}

        def layer(i, x):
            tiles = [None] * ((TY + 2 * HY) // BY)
            for bx in range(NBX):
                if not 0 <= x - bx * BX < WX:
                    continue
                for by in range(NBY):
                    rows = XP[bx * NBY + by, i, starts[bx, by] + (x - bx * BX)]
                    for q in range(WY // BY):
                        part = rows[q * BY:(q + 1) * BY]
                        old = tiles[by + q]
                        tiles[by + q] = part if old is None else old + part
            return jnp.concatenate(tiles, axis=0)

        for g in range(EG):
            above, below = packed(functools.partial(layer, 1), g)
            ACC[EX + EG + g] = above
            ACC[EX + g] = below
        for x in range(EX):
            ACC[x] = layer(0, x)

    def return_exchange(ACC, k, between):
        copies = []
        for n, way in enumerate(WAYS):
            copies.append((way, back[n].at[k], Copy(
                rim(ACC, way[2], region(way, piece)), back[n].at[k], way).start()))
        between()
        SUM[...] = jnp.zeros_like(SUM)
        for way, came, copy in copies:
            copy.landed()
            other = tuple(-w for w in way)
            xs, ys = region(other, border)
            if way[2]:
                side = 0 if way[2] > 0 else 1
                SUM[side, xs, ys, :] = SUM[side, xs, ys, :] + came[...]
            else:
                ACC[xs, ys, :] = ACC[xs, ys, :] + came[...]
        for g in range(G):
            first, last = SUM[0, XG + g, OY, :], SUM[1, XG + g, OY, :]
            for j in range(PK):
                x = PK * g + j
                edge = jnp.logical_or(lane2 < HZ, lane2 >= LANES - HZ)
                ADJ[x] = ACC[HX + x, OY, :] + jnp.where(edge, unpacked(first, last, j), 0.0)

    def each_block(fn):
        for bx in range(NBX):
            for by in range(NBY):
                fn(bx, by)

    for load in loads:
        load.wait()
    E0[OX, OY, :] = STEP_SIZE * sum(grad[0, c].astype(jnp.float32) * vel[c] for c in range(3))
    pack_own(E0, 0)
    pl.semaphore_wait(barrier, total)

    def prepare():
        for ref in (YP, XP):
            ref[...] = jnp.zeros_like(ref)
        send_faces()

    def nothing():
        pass

    faces = []

    def send_faces():
        VE[:, LH:LH + TX, OY, :] = vel[...]
        for c in range(3):
            for i in range(TX // 2):
                for h in range(2):
                    YSU[c, i, LH * h:LH * (h + 1), :] = vel[c, 2 * i + h, TY - LH:TY, :]
                    YSD[c, i, LH * h:LH * (h + 1), :] = vel[c, 2 * i + h, 0:LH, :]
            for g in range(TX // VPK):
                row = None
                for j in range(VPK):
                    turned = pltpu.roll(vel[c, VPK * g + j], (2 * LH * j + LH) % LANES, 1)
                    row = turned if row is None else jnp.where(lane2 // (2 * LH) == j, turned, row)
                SV[c, g] = row
        faces.extend([
            Copy(SV, VRD, (0, 0, 1)).start(), Copy(SV, VRU, (0, 0, -1)).start(),
            Copy(vel.at[:, TX - LH:TX], VE.at[:, 0:LH, OY, :], (1, 0, 0)).start(),
            Copy(vel.at[:, 0:LH], VE.at[:, LH + TX:2 * LH + TX, OY, :], (-1, 0, 0)).start(),
            Copy(YSU, YVD, (0, 1, 0)).start(), Copy(YSD, YVU, (0, -1, 0)).start()])

    forward_exchange(E0, 0, prepare)
    unpack(E0)

    def first(bx, by):
        y0 = by * BY
        ST[pl.ds(bx * BX, BX), pl.ds(y0, BY), :] = gather_block(E0, 0, bx, by)

    each_block(first)
    g1 = sum(grad[1, c].astype(jnp.float32) * vel[c] for c in range(3))
    E1[OX, OY, :] = ST[...] + STEP_SIZE * g1
    pack_own(E1, 1)

    forward_exchange(E1, 1, nothing)
    unpack(E1)

    def second(bx, by):
        spread_block(gather_block(E1, 1, bx, by), 1, bx, by)

    each_block(second)
    collect(ACC1, 1)

    def regular():
        for f in faces:
            f.landed()
        for c in range(3):
            for i in range(TX // 2):
                for h in range(2):
                    VE[c, LH + 2 * i + h, HY - LH:HY, :] = YVD[c, i, LH * h:LH * (h + 1), :]
                    VE[c, LH + 2 * i + h, HY + TY:HY + TY + LH, :] = YVU[c, i, LH * h:LH * (h + 1), :]
        rows = lax.broadcasted_iota(jnp.int32, (2 * LANES, LANES), 0)
        cols = lax.broadcasted_iota(jnp.int32, (2 * LANES, LANES), 1)
        r = rows - LANES
        place = jnp.where(rows < LANES, rows, jnp.where(r < LH, r + LANES, r - LANES))
        known = jnp.logical_or(rows < LANES, jnp.logical_or(r < LH, r >= LANES - LH))
        gap = jnp.abs(place - cols)
        band = jnp.zeros((2 * LANES, LANES), jnp.float32)
        for k in range(5):
            tap = (3.0 if k == 0 else 1.0) * LAPLACE_TAPS[k]
            band = jnp.where(jnp.logical_and(known, gap == k), tap, band)
        for c in range(3):
            rims = []
            for g in range(TX // VPK):
                row = jnp.where(lane2 % (2 * LH) < LH, VRD[c, g], VRU[c, g])
                for j in range(VPK):
                    rims.append(pltpu.roll(row, (LANES - (2 * LH * j + LH)) % LANES, 1))
            rim = jnp.concatenate(rims, axis=0)
            own = vel[c].reshape(TX * TY, LANES)
            res = jnp.dot(jnp.concatenate([own, rim], axis=1), band,
                          preferred_element_type=jnp.float32,
                          precision=lax.Precision.HIGHEST).reshape(TX, TY, LANES)
            for k in range(1, 5):
                res = res + LAPLACE_TAPS[k] * (
                    VE[c, LH + k:LH + k + TX, OY, :] + VE[c, LH - k:LH - k + TX, OY, :]
                    + VE[c, LH:LH + TX, HY + k:HY + k + TY, :]
                    + VE[c, LH:LH + TX, HY - k:HY - k + TY, :])
            out[c] = (-REG_WEIGHT) * res

    return_exchange(ACC1, 1, regular)

    def third(bx, by):
        y0 = by * BY
        vals = ADJ[pl.ds(bx * BX, BX), pl.ds(y0, BY), :]
        spread_block(vals, 0, bx, by)

    each_block(third)
    collect(ACC0, 0)

    def add_gauss(k):
        for c in range(3):
            out[c] = out[c] + STEP_SIZE * grad[k, c].astype(jnp.float32) * ADJ[...]

    def last():
        add_gauss(1)
        for copy in sends:
            copy.left()

    return_exchange(ACC0, 0, last)
    add_gauss(0)


COPIES = 4 * len(WAYS) + 6


def body(shape, velocity, gradients, shift_x, shift_y, shift_z, fractions):
    TX, TY, TZ = velocity.shape[1:]
    assert TZ == BZ == LANES and TX % VPK == 0 and TX % BX == 0 and TY % BY == 0
    EX, EY = TX + 2 * HX, TY + 2 * HY
    EG, G = EX // PK, TX // PK
    NB = (TX // BX) * (TY // BY)

    def span(way):
        groups = (XG if way[0] else G) if way[2] else (HX if way[0] else TX)
        return groups, HY if way[1] else TY

    vm = lambda *s: pltpu.VMEM(s, jnp.float32)
    vmem = pl.BlockSpec(memory_space=pltpu.VMEM)
    hbm = pl.BlockSpec(memory_space=pltpu.HBM)
    shift_x, shift_y, shift_z = (s.transpose(0, 1, 3, 2) for s in (shift_x, shift_y, shift_z))
    fractions = fractions.transpose(0, 2, 3, 4, 1)
    return pl.pallas_call(
        functools.partial(kernel, shape),
        out_shape=jax.ShapeDtypeStruct(velocity.shape, jnp.float32),
        in_specs=[hbm] * 6,
        out_specs=vmem,
        scratch_shapes=[
            pltpu.VMEM(velocity.shape, velocity.dtype), pltpu.VMEM(gradients.shape, gradients.dtype),
            *[pltpu.SMEM(s.shape, s.dtype) for s in (shift_x, shift_y, shift_z, fractions)],
            pltpu.SemaphoreType.DMA((6,)),
            vm(EX + 2 * EG, EY, LANES), vm(EX + 2 * EG, EY, LANES),
            vm(EX, EY, LANES),
            vm(NB, 2 * BX, 2 * WY - BY, LANES), vm(NB, 2, 2 * WX - BX, WY, LANES),
            vm(EX + 2 * EG, EY, LANES), vm(EX + 2 * EG, EY, LANES),
            vm(NB, 2 * BX, WY, LANES), vm(TX, TY, LANES), vm(TX, TY, LANES),
            vm(2, 2, EG, EY, LANES), vm(2, EG, EY, LANES),
            vm(3, TX + 2 * LH, EY, LANES),
            vm(3, TX // 2, 2 * LH, LANES), vm(3, TX // 2, 2 * LH, LANES),
            vm(3, TX // 2, 2 * LH, LANES), vm(3, TX // 2, 2 * LH, LANES),
            vm(3, TX // VPK, TY, LANES), vm(3, TX // VPK, TY, LANES), vm(3, TX // VPK, TY, LANES),
            *[vm(2, *span(way), LANES) for way in WAYS],
            pltpu.SemaphoreType.DMA((COPIES,)), pltpu.SemaphoreType.DMA((COPIES,)),
        ],
        compiler_params=pltpu.CompilerParams(collective_id=0, has_side_effects=True,
                                             vmem_limit_bytes=16 << 20),
    )(*(pltpu.with_memory_space_constraint(x, pltpu.HBM) for x in (velocity, gradients, shift_x, shift_y, shift_z, fractions)))


def solution(mesh):
    in_specs = (
        P(None, "gx", "gy", "gz"),
        P(None, None, "gx", "gy", "gz"),
        P(None, "gx", "gy", "gz"),
        P(None, "gx", "gy", "gz"),
        P(None, "gx", "gy", "gz"),
        P(None, None, "gx", "gy", "gz"),
    )
    out_specs = P(None, "gx", "gy", "gz")
    return jax.shard_map(functools.partial(body, dict(mesh.shape)), mesh=mesh, in_specs=in_specs,
                         out_specs=out_specs, check_vma=False)
```
